32 devices in a mesh: expert: 8 (over y, x, core), shard: 4 (over z).
Axes of the slice: x: 2, y: 2, z: 4, core: 2. Of those that a mesh axis runs over, the one named last changes fastest.
Arguments:
- inputs: bfloat16 [6304, 768], P(('expert', 'shard')), may hold values from -6 to 6
- routes: int32 [6304, 2], P(('expert', 'shard')), may hold values from 0 to 15, all different within a row; in each aligned block of 197 rows (0 to 196, 197 to 393, ...) at most 39 rows name the same one
- ln1_gain: bfloat16 [768], P(('expert', 'shard')), may hold values from 0.099609375 to 1.8984375
- ln1_bias: bfloat16 [768], P(('expert', 'shard')), may hold values from -3 to 3
- w_qkv: bfloat16 [768, 2304], P(('expert', 'shard')), may hold values from -0.21875 to 0.21875
- w_attn_out: bfloat16 [768, 768], P(('expert', 'shard')), may hold values from -0.625 to 0.625
- ln2_gain: bfloat16 [768], P(('expert', 'shard')), may hold values from 0.099609375 to 1.8984375
- ln2_bias: bfloat16 [768], P(('expert', 'shard')), may hold values from -3 to 3
- w_router: bfloat16 [768, 16], P(('expert', 'shard')), may hold values from -0.109375 to 0.109375
- w_in: bfloat16 [16, 768, 3072], P('expert', None, 'shard'), may hold values from -0.21875 to 0.21875
- w_expert_out: bfloat16 [16, 3072, 768], P('expert', 'shard'), may hold values from -1.25 to 1.25
- cotangent: bfloat16 [6304, 768], P(('expert', 'shard')), may hold values from -6 to 6
Outputs:
- outputs: bfloat16 [6304, 768], P(('expert', 'shard'))
- grad_inputs: float32 [6304, 768], P(('expert', 'shard'))
- grad_ln1_gain: float32 [768], P(('expert', 'shard'))
- grad_ln1_bias: float32 [768], P(('expert', 'shard'))
- grad_w_qkv: float32 [768, 2304], P(('expert', 'shard'))
- grad_w_attn_out: float32 [768, 768], P(('expert', 'shard'))
- grad_ln2_gain: float32 [768], P(('expert', 'shard'))
- grad_ln2_bias: float32 [768], P(('expert', 'shard'))
- grad_w_router: float32 [768, 16], P(('expert', 'shard'))
- grad_w_in: float32 [16, 768, 3072], P('expert', None, 'shard')
- grad_w_expert_out: float32 [16, 3072, 768], P('expert', 'shard')
The draws below stay inside these ranges and needn't reach their ends.
Inputs may be any that keep to these rules, and one draw needn't show every extreme that they name: `routes`: each token names two different experts; among the 197 tokens of one device no expert is named more than 39 times, and in every draw some expert is named exactly 39 times by one device's tokens.
All inputs are finite; a program needn't handle non-finite values.
Results may differ from the reference program's by a relative error of at most 0.018.
Values may be sent and summed in bfloat16 or wider, within the bound.
No kernel may reach another device: no remote copies, remote signals or barrier semaphores. Data moves between devices by JAX's collectives and lax.ppermute only.
A program may use at most 192 MiB of HBM per device.

```python
import math
from functools import partial
import jax
import jax.numpy as jnp
import numpy as np
from jax import lax

D = 768
HEADS = 12
HEAD_DIM = 64
FF = 3072
SEQ = 197
IMG_DEV = 1
ROWS = 197
E = 16
CAP = 39
TOKENS = 6304
N_SHARD = 4
DEVICES = 32


def raised(values, key, source, target, shards_of, factor):
    def block_of(dim):
        return (jnp.arange(values.shape[dim]) // (values.shape[dim] // shards_of)).reshape((-1,) + (1,) * (values.ndim - 1 - dim))

    one_side = jax.random.permutation(key, shards_of)[block_of(target)]
    second = (block_of(target) + shards_of // 2) % shards_of
    return jnp.where((block_of(source) == one_side) | (block_of(source) == second), factor * values, values)


def level_of(own_key, extent, cuts, smallest, high):
    loudness = 1.0
    for dim, blocks in cuts:
        draws = jax.random.uniform(jax.random.fold_in(jax.random.fold_in(own_key, 6), dim), (blocks,), jnp.float32, smallest / len(cuts), high / len(cuts))
        loudness = loudness * jnp.repeat(jnp.exp(draws), extent[dim] // blocks).reshape((-1,) + (1,) * (len(extent) - 1 - dim))
    return loudness


def assign_block(stream_key, own, number, rows, number_of, top, limit, slope):
    sequence = jax.random.permutation(stream_key, number_of)
    heavy_load, ordinary = shares(number_of, rows * top, limit, slope, True), shares(number_of, rows * top, limit, slope, False)
    places = jnp.arange(number_of)

    def named(lengths, turn):
        used = int((lengths > 0).sum())
        fixed = max(1, used // 4)
        shifted = fixed + (places - fixed + turn * (used - fixed)) % max(1, number_of - fixed)
        return jnp.zeros((number_of,), jnp.int32).at[sequence[jnp.where(places < fixed, places, shifted)]].set(jnp.asarray(lengths, jnp.int32))

    lengths = jnp.where(number % 4 == 0, named(heavy_load, number // 4), named(ordinary, number - number // 4 - 1))
    mixed = jax.random.permutation(jax.random.fold_in(own, 3), number_of)
    source_of, receiver = mixed[0:number_of // 2 * 2:2], mixed[1:number_of // 2 * 2:2]
    slack = jnp.minimum(lengths[source_of] - 1, limit - lengths[receiver]) // 2
    slack = jnp.where((source_of == sequence[0]) | (receiver == sequence[0]) | (lengths[receiver] == 0), 0, jnp.maximum(slack, 0))
    shifted = jax.random.randint(jax.random.fold_in(own, 4), (number_of // 2,), 0, 1 << 20) % (slack + 1)
    lengths = lengths.at[source_of].add(-shifted).at[receiver].add(shifted)
    items = jnp.searchsorted(jnp.cumsum(lengths), jnp.arange(rows * top), side="right").astype(jnp.int32)
    listing = items.reshape(top, rows).T
    listing = listing[jax.random.permutation(jax.random.fold_in(own, 1), rows)]
    turn = jax.random.randint(jax.random.fold_in(own, 2), (rows, 1), 0, top)
    return jnp.take_along_axis(listing, (jnp.arange(top)[None, :] + turn) % top, axis=1)


def shares(count, total, bound, slope, full):
    portions = [(1 << 20) // math.isqrt(standing ** slope) + 1 for standing in range(1, count + 1)]
    largest = bound if full else min(bound, max(-(-total // count), total * portions[0] // sum(portions)))
    least = 1 if total - largest >= count - 1 else 0
    holding, rest = [largest] + [least] * (count - 1), total - largest - least * (count - 1)
    while rest > 0:
        movable = [i for i in range(1, count) if holding[i] < largest] or [i for i in range(1, count) if holding[i] < bound]
        mass, budget = sum([portions[i] for i in movable]), rest
        for i in movable:
            addition = min(bound - holding[i], max(1, budget * portions[i] // mass), rest)
            holding[i] = holding[i] + addition
            rest = rest - addition
    return np.array(holding)


def bell_draw(own_key, shape, deviation, reach, shards=(), held_as=jnp.bfloat16):
    drawn = jax.random.normal(own_key, shape, jnp.float32) * deviation
    if len(shards) > 0:
        drawn = level_of(own_key, shape, shards, -0.22, 0.18) * drawn
    return jnp.clip(drawn, min=-reach, max=reach).astype(held_as)


def noise_with(key, dims, deviation, reach, shards, heavy, kind=jnp.bfloat16):
    result = deviation * jax.random.normal(key, dims, jnp.float32)
    if shards:
        result = result * level_of(key, dims, shards, -0.22, 0.18)
    return jnp.clip(raised(result, jax.random.fold_in(key, 3), *heavy), -reach, reach).astype(kind)


def setup_inputs(seed: int = 0) -> dict:
    seeds = jax.random.split(jax.random.key(seed), 13)
    inputs = bell_draw(seeds[0], (TOKENS, D), 1.0, 6.0, ((0, 32),))
    routes_keys = jax.random.split(jax.random.fold_in(seeds[1], 1), TOKENS // ROWS)
    routes_turns = jax.random.permutation(jax.random.fold_in(seeds[1], 3), TOKENS // ROWS)
    routes = jax.vmap(lambda own, number: assign_block(jax.random.fold_in(seeds[1], 2), own, number, ROWS, E, 2, CAP, 2))(routes_keys, routes_turns).reshape((TOKENS, 2))
    ln1_gain = jnp.clip(1.0 + 0.18 * jax.random.normal(seeds[2], (D,), jnp.float32), 0.099609375, 1.8984375).astype(jnp.bfloat16)
    ln1_bias = bell_draw(seeds[3], (D,), 0.5, 3.0, ((0, 32),))
    w_qkv = bell_draw(seeds[4], (D, 3 * D), D ** -0.5, 0.21875, ((0, 32),))
    w_attn_out = bell_draw(seeds[5], (D, D), (D // 8) ** -0.5, 0.625, ((0, 32),))
    ln2_gain = jnp.clip(1.0 + 0.18 * jax.random.normal(seeds[6], (D,), jnp.float32), 0.099609375, 1.8984375).astype(jnp.bfloat16)
    ln2_bias = bell_draw(seeds[7], (D,), 0.5, 3.0, ((0, 32),))
    w_router = bell_draw(seeds[8], (D, E), (4 * D) ** -0.5, 0.109375, ((0, 32),))
    w_in = bell_draw(seeds[9], (E, D, FF), D ** -0.5, 0.21875, ((0, 8), (2, 4)))
    w_expert_out = bell_draw(seeds[10], (E, FF, D), (max(1, 2 * FF // (E * E))) ** -0.5, 1.25, ((0, 8), (1, 4)))
    cotangent = noise_with(seeds[11], (TOKENS, D), 1.0, 6.0, ((0, 32),), (0, 1, 32, 2.75))
    return dict(inputs=inputs, routes=routes, ln1_gain=ln1_gain, ln1_bias=ln1_bias, w_qkv=w_qkv, w_attn_out=w_attn_out, ln2_gain=ln2_gain, ln2_bias=ln2_bias, w_router=w_router, w_in=w_in, w_expert_out=w_expert_out, cotangent=cotangent)


EPS = 1e-06

def to_narrow(values):
    return lax.optimization_barrier(values.astype(jnp.bfloat16))

def layer_norm(values, gain_vec, bias_vec):
    average = lax.optimization_barrier(jnp.mean(values, axis=-1, keepdims=True))
    centred = values - average
    inverse = lax.rsqrt(lax.optimization_barrier(jnp.mean(centred * centred, axis=-1, keepdims=True)) + EPS)
    unit_vals = centred * inverse
    return (unit_vals * gain_vec + bias_vec, unit_vals, inverse)

def norm_back(grad_out, unit_vals, inverse, gain_vec):
    scaled = grad_out * gain_vec
    centred = scaled - lax.optimization_barrier(jnp.mean(scaled, axis=-1, keepdims=True)) - unit_vals * lax.optimization_barrier(jnp.mean(scaled * unit_vals, axis=-1, keepdims=True))
    return (inverse * centred, lax.optimization_barrier(jnp.sum(grad_out * unit_vals, axis=0)), lax.optimization_barrier(jnp.sum(grad_out, axis=0)))

def split_heads(packed):
    shaped = packed.reshape(packed.shape[0], packed.shape[1], 3, HEADS, HEAD_DIM)
    return (shaped[:, :, 0], shaped[:, :, 1], shaped[:, :, 2])

def attn_probs(queries, keys_part):
    scores = jnp.einsum('iqhd,ikhd->ihqk', queries.astype(jnp.float32), keys_part.astype(jnp.float32)) * HEAD_DIM ** (-0.5)
    exponent = jnp.exp(scores)
    return exponent / lax.optimization_barrier(jnp.sum(exponent, axis=-1, keepdims=True))

def attention_forward(packed):
    queries, keys_part, values_part = split_heads(packed)
    probs_b = to_narrow(attn_probs(queries, keys_part))
    context = jnp.einsum('ihqk,ikhd->iqhd', probs_b.astype(jnp.float32), values_part.astype(jnp.float32))
    return context.astype(jnp.bfloat16).reshape(packed.shape[0], packed.shape[1], HEADS * HEAD_DIM)

def attention_backward(pair_args):
    packed, d_context = pair_args
    queries, keys_part, values_part = split_heads(packed)
    probs = attn_probs(queries, keys_part)
    probs_b = to_narrow(probs)
    d_heads = d_context.reshape(packed.shape[0], packed.shape[1], HEADS, HEAD_DIM).astype(jnp.float32)
    d_values = jnp.einsum('ihqk,iqhd->ikhd', probs_b.astype(jnp.float32), d_heads)
    d_probs = jnp.einsum('iqhd,ikhd->ihqk', d_heads, values_part.astype(jnp.float32))
    row_dot = lax.optimization_barrier(jnp.sum(probs * d_probs, axis=-1, keepdims=True))
    d_scores = to_narrow(probs * (d_probs - row_dot)).astype(jnp.float32)
    scale = HEAD_DIM ** (-0.5)
    d_queries = jnp.einsum('ihqk,ikhd->iqhd', d_scores, keys_part.astype(jnp.float32)) * scale
    d_keys = jnp.einsum('ihqk,iqhd->ikhd', d_scores, queries.astype(jnp.float32)) * scale
    stacked = jnp.stack([d_queries, d_keys, d_values], axis=2)
    return stacked.astype(jnp.bfloat16).reshape(packed.shape[0], packed.shape[1], 3 * HEADS * HEAD_DIM)

def grouped_sum(left, right):
    rows = left.shape[0]
    left_groups = left.reshape(rows, N_SHARD, -1).astype(jnp.float32)
    right_groups = right.reshape(N_SHARD, -1, right.shape[-1]).astype(jnp.float32)
    partials = jnp.einsum('mnf,nfd->nmd', left_groups, right_groups)
    return lax.optimization_barrier(jnp.sum(to_narrow(partials).astype(jnp.float32), axis=0)).astype(jnp.bfloat16)

def reference(inputs, routes, ln1_gain, ln1_bias, w_qkv, w_attn_out, ln2_gain, ln2_bias, w_router, w_in, w_expert_out, cotangent):
    gain_one = ln1_gain.astype(jnp.float32)
    gain_two = ln2_gain.astype(jnp.float32)
    features = inputs.astype(jnp.float32)
    normed1, unit_one, inverse_one = layer_norm(features, gain_one, ln1_bias.astype(jnp.float32))
    narrow_one = normed1.astype(jnp.bfloat16)
    packed = jnp.dot(narrow_one, w_qkv, preferred_element_type=jnp.float32).astype(jnp.bfloat16)
    packed_blocks = packed.reshape(DEVICES, IMG_DEV, SEQ, 3 * D)
    context = lax.map(attention_forward, packed_blocks).reshape(TOKENS, D)
    hidden = features + jnp.dot(context, w_attn_out, preferred_element_type=jnp.float32)
    normed2, unit_two, inverse_two = layer_norm(hidden, gain_two, ln2_bias.astype(jnp.float32))
    narrow_two = normed2.astype(jnp.bfloat16)
    logits = jnp.dot(narrow_two, w_router, preferred_element_type=jnp.float32)
    exponent = jnp.exp(logits)
    router_probs = exponent / lax.optimization_barrier(jnp.sum(exponent, axis=-1, keepdims=True))
    route_table = (routes[:, :, None] == jnp.arange(E, dtype=jnp.int32)[None, None, :]).astype(jnp.float32)
    gate_vals = lax.optimization_barrier(jnp.sum(route_table * router_probs[:, None, :], axis=-1))
    grad_out = cotangent.astype(jnp.float32)
    flat_routes = routes.reshape(-1)
    assigned = flat_routes.shape[0]
    most_load = DEVICES * CAP
    slot_range = jnp.arange(most_load, dtype=jnp.int32)
    assign_range = jnp.arange(assigned, dtype=jnp.int32)
    d_expert_flat = (gate_vals[:, :, None] * grad_out[:, None, :]).astype(jnp.bfloat16).reshape(assigned, D)
    gelu_fn = partial(jax.nn.gelu, approximate=True)

    def one_expert(carried, expert_slice):
        out_flat, back_flat = carried
        expert_id, weight_in, weight_out = expert_slice
        member = flat_routes == expert_id
        position = jnp.cumsum(member.astype(jnp.int32)) - 1
        live_count = jnp.sum(member.astype(jnp.int32))
        target = jnp.where(member, position, most_load).astype(jnp.int32)
        slot_source = jnp.zeros((most_load,), jnp.int32).at[target].set(assign_range, mode='drop')
        live = slot_range < live_count
        gathered = jnp.where(live[:, None], narrow_two[slot_source // 2], jnp.zeros((), jnp.bfloat16))
        grad_rows = jnp.where(live[:, None], d_expert_flat[slot_source], jnp.zeros((), jnp.bfloat16))
        pre_act = jnp.dot(gathered, weight_in, preferred_element_type=jnp.float32)
        hidden_act = gelu_fn(pre_act).astype(jnp.bfloat16)
        expert_rows = grouped_sum(hidden_act, weight_out)
        d_hidden_act = jnp.dot(grad_rows, weight_out.T, preferred_element_type=jnp.float32)
        _, pullback = jax.vjp(gelu_fn, pre_act)
        d_pre = pullback(d_hidden_act)[0].astype(jnp.bfloat16)
        grad_in_g = jnp.dot(gathered.T, d_pre, preferred_element_type=jnp.float32)
        grad_out_g = jnp.dot(hidden_act.T, grad_rows, preferred_element_type=jnp.float32)
        back_rows = grouped_sum(d_pre, weight_in.T)
        destination = jnp.where(live, slot_source, assigned).astype(jnp.int32)
        out_flat = out_flat.at[destination].set(expert_rows, mode='drop')
        back_flat = back_flat.at[destination].set(back_rows, mode='drop')
        return ((out_flat, back_flat), (grad_in_g, grad_out_g))
    start_flat = jnp.zeros((assigned, D), jnp.bfloat16)
    (out_flat, back_flat), (grad_w_in, grad_w_expert_out) = lax.scan(one_expert, (start_flat, start_flat), (jnp.arange(E, dtype=jnp.int32), w_in, w_expert_out))
    expert_vals = out_flat.reshape(TOKENS, 2, D).astype(jnp.float32)
    outputs = (hidden + lax.optimization_barrier(jnp.sum(gate_vals[:, :, None] * expert_vals, axis=1))).astype(jnp.bfloat16)
    d_gate = lax.optimization_barrier(jnp.sum(expert_vals * grad_out[:, None, :], axis=-1))
    d_probs = lax.optimization_barrier(jnp.sum(route_table * d_gate[:, :, None], axis=1))
    d_logits = router_probs * (d_probs - lax.optimization_barrier(jnp.sum(router_probs * d_probs, axis=-1, keepdims=True)))
    grad_w_router = jnp.dot(narrow_two.astype(jnp.float32).T, d_logits, precision=lax.Precision.HIGHEST)
    back_vals = back_flat.reshape(TOKENS, 2, D).astype(jnp.float32)
    d_normed2 = back_vals[:, 0] + back_vals[:, 1] + jnp.dot(d_logits, w_router.astype(jnp.float32).T, precision=lax.Precision.HIGHEST)
    d_norm_two, grad_ln2_gain, grad_ln2_bias = norm_back(d_normed2, unit_two, inverse_two, gain_two)
    d_hidden = grad_out + d_norm_two
    d_hidden_b = d_hidden.astype(jnp.bfloat16)
    grad_w_attn_out = jnp.dot(context.T, d_hidden_b, preferred_element_type=jnp.float32)
    d_context = jnp.dot(d_hidden_b, w_attn_out.T, preferred_element_type=jnp.float32).astype(jnp.bfloat16)
    d_packed = lax.map(attention_backward, (packed_blocks, d_context.reshape(DEVICES, IMG_DEV, SEQ, D))).reshape(TOKENS, 3 * D)
    grad_w_qkv = jnp.dot(narrow_one.T, d_packed, preferred_element_type=jnp.float32)
    d_normed1 = jnp.dot(d_packed, w_qkv.T, preferred_element_type=jnp.float32)
    d_norm_one, grad_ln1_gain, grad_ln1_bias = norm_back(d_normed1, unit_one, inverse_one, gain_one)
    grad_inputs = d_hidden + d_norm_one
    return (outputs, grad_inputs, grad_ln1_gain, grad_ln1_bias, grad_w_qkv, grad_w_attn_out, grad_ln2_gain, grad_ln2_bias, grad_w_router, grad_w_in, grad_w_expert_out)
```

```python
import math

import jax
import jax.numpy as jnp
from jax import lax
from jax.experimental import pallas as pl
from jax.experimental.pallas import tpu as pltpu
from jax.sharding import PartitionSpec as P

HEADS = 12
HEAD_DIM = 64
EXP_DEV = 2
SEQ = 197
EPS = 1e-06
AXES = ("expert", "shard")
BF = jnp.bfloat16
F32 = jnp.float32
GELU_C = math.sqrt(2.0 / math.pi)
GELU_A = 0.044715


def round_up(n, m):
    return -(-n // m) * m


def swap_expert(x, mask):
    ne, ns = lax.axis_size("expert"), lax.axis_size("shard")
    return lax.ppermute(x, AXES, [(e * ns + s, (e ^ mask) * ns + s) for e in range(ne) for s in range(ns)])


def move_shard(x, moves):
    ne, ns = lax.axis_size("expert"), lax.axis_size("shard")
    return lax.ppermute(x, AXES, [(e * ns + s, e * ns + d) for e in range(ne) for s, d in moves])


SWAP = ((0, 1), (1, 0), (2, 3), (3, 2))
MID = ((1, 2), (2, 1))
OUT = ((1, 0), (2, 3))
IN = ((0, 1), (3, 2))


def shard_is_inner():
    s = lax.axis_index("shard")
    return (s == 1) | (s == 2)


def gather_shard(x, direct=False):
    ns = lax.axis_size("shard")
    if direct:
        return [x] + [move_shard(x, [(s, s ^ m) for s in range(ns)]) for m in range(1, ns)]
    if ns == 4:
        near = move_shard(x, SWAP)
        mid = move_shard(x, MID)
        far_out = move_shard(mid, OUT)
        far_in = move_shard(near, MID)
        end = move_shard(far_in, OUT)
        inner = shard_is_inner()
        return [x, near, jnp.where(inner, far_in, far_out), jnp.where(inner, mid, end)]
    parts = [x]
    for b in range(ns.bit_length() - 1):
        step = 1 << b
        moves = [(s, s ^ step) for s in range(ns)]
        parts = parts + [move_shard(v, moves) for v in parts]
    return parts


def add(a, b):
    return (a.astype(F32) + b.astype(F32)).astype(a.dtype)


def scatter_shard(parts, direct=False):
    ns = lax.axis_size("shard")
    if direct:
        total = parts[0].astype(F32)
        for m in range(1, ns):
            total += move_shard(parts[m], [(s, s ^ m) for s in range(ns)]).astype(F32)
        return total
    if ns == 4:
        p0, p1, p2, p3 = parts
        t = move_shard(p3, IN)
        r1 = move_shard(p2, IN)
        r2 = move_shard(add(p2, t), MID)
        q = move_shard(add(p3, r1), MID)
        near = move_shard(add(p1, r2), SWAP)
        return (p0.astype(F32) + q.astype(F32)) + near.astype(F32)
    for b in reversed(range(ns.bit_length() - 1)):
        step = 1 << b
        moves = [(s, s ^ step) for s in range(ns)]
        half = len(parts) // 2
        parts = [add(parts[i], move_shard(parts[half + i], moves)) for i in range(half)]
    return parts[0].astype(F32)


def high_bits():
    return list(range(1, lax.axis_size("expert").bit_length() - 1))


def pair_orders():
    ns = lax.axis_size("shard")
    return [((2 * k, high_bits()), (2 * k + 1, high_bits()[::-1])) for k in range(ns // 2)]


def gather_plane(x, direct=False):
    parts = gather_shard(x, direct)
    chunks = []
    for pair in pair_orders():
        pieces = []
        for slot, order in pair:
            block = parts[slot][None]
            for b in order[:-1]:
                block = jnp.concatenate([block, swap_expert(block, 1 << b)], axis=0)
            pieces += [block, swap_expert(block, 1 << order[-1])]
        chunks.append(pieces)
    return chunks


def gather_core(chunks, in_turn=False):
    done = []
    for pieces in chunks:
        if in_turn and done:
            pieces, _ = lax.optimization_barrier((pieces, done[-1]))
        done.append(list(pieces) + [swap_expert(p, 1) for p in pieces])
    return done


def chunk_labels():
    chunks = []
    for pair in pair_orders():
        pieces = []
        for slot, order in pair:
            block = [(0, slot)]
            for b in order[:-1]:
                block = block + [(e ^ (1 << b), z) for e, z in block]
            pieces += [block, [(e ^ (1 << order[-1]), z) for e, z in block]]
        chunks.append(pieces + [[(e ^ 1, z) for e, z in p] for p in pieces])
    return chunks


def scatter_chunk(pieces, k):
    half = len(pieces) // 2
    own = [add(pieces[i], swap_expert(pieces[half + i], 1)) for i in range(half)]
    parts = []
    for i, (_, order) in enumerate(pair_orders()[k]):
        block = add(own[2 * i], swap_expert(own[2 * i + 1], 1 << order[-1]))
        for b in reversed(order[:-1]):
            h = block.shape[0] // 2
            block = add(block[:h], swap_expert(block[h:], 1 << b))
        parts.append(block[0])
    return parts


def scatter_plane(chunks):
    parts = []
    for k, pieces in enumerate(chunks):
        parts += scatter_chunk(pieces, k)
    return parts


def slot_devices():
    ns = lax.axis_size("shard")
    e, s = lax.axis_index("expert"), lax.axis_index("shard")
    labels = [lab for pieces in chunk_labels() for p in pieces for lab in p]
    le = jnp.array([a for a, _ in labels], jnp.int32)
    ls = jnp.array([b for _, b in labels], jnp.int32)
    return (le ^ e) * ns + (ls ^ s)


def place_blocks(pieces, where, blocks, widths):
    count = len(pieces)
    rows = pieces[0].shape[1]

    def kernel(where_ref, *refs):
        outs, sems = refs[count : count + len(widths)], refs[count + len(widths)]
        copies, i = [], 0
        for p in refs[:count]:
            for k in range(p.shape[0]):
                start = 0
                for c, w in enumerate(widths):
                    copies.append(
                        pltpu.make_async_copy(
                            p.at[k, :, pl.ds(start, w)], outs[c].at[where_ref[i]], sems.at[c, i]
                        )
                    )
                    start += w
                i += 1
        for c in copies:
            c.start()
        for c in copies:
            c.wait()

    vmem = pl.BlockSpec(memory_space=pltpu.VMEM)
    return pl.pallas_call(
        kernel,
        out_shape=tuple(jax.ShapeDtypeStruct((blocks, rows, w), pieces[0].dtype) for w in widths),
        in_specs=[pl.BlockSpec(memory_space=pltpu.SMEM)] + [pl.BlockSpec(memory_space=pl.ANY)] * count,
        out_specs=tuple([vmem] * len(widths)),
        scratch_shapes=[pltpu.SemaphoreType.DMA((len(widths), blocks))],
        name="place_blocks",
    )(where, *pieces)


def take_blocks(tables, where, sizes):
    count, given = len(sizes), len(tables)
    blocks, rows = tables[0].shape[:2]
    widths = [t.shape[2] for t in tables]

    def kernel(where_ref, *refs):
        tabs, outs, sems = refs[:given], refs[given : given + count], refs[given + count]
        copies, i = [], 0
        for p in outs:
            for k in range(p.shape[0]):
                start = 0
                for c, w in enumerate(widths):
                    copies.append(
                        pltpu.make_async_copy(
                            tabs[c].at[where_ref[i]], p.at[k, :, pl.ds(start, w)], sems.at[c, i]
                        )
                    )
                    start += w
                i += 1
        for c in copies:
            c.start()
        for c in copies:
            c.wait()

    vmem = pl.BlockSpec(memory_space=pltpu.VMEM)
    return pl.pallas_call(
        kernel,
        out_shape=tuple(jax.ShapeDtypeStruct((n, rows, sum(widths)), tables[0].dtype) for n in sizes),
        in_specs=[pl.BlockSpec(memory_space=pltpu.SMEM)] + [pl.BlockSpec(memory_space=pl.ANY)] * given,
        out_specs=tuple([vmem] * count),
        scratch_shapes=[pltpu.SemaphoreType.DMA((given, blocks))],
        name="take_blocks",
    )(where, *tables)


def layer_norm(values, gain_vec, bias_vec):
    average = jnp.mean(values, axis=-1, keepdims=True)
    centred = values - average
    inverse = lax.rsqrt(jnp.mean(centred * centred, axis=-1, keepdims=True) + EPS)
    unit_vals = centred * inverse
    return (unit_vals * gain_vec + bias_vec, unit_vals, inverse)


def norm_back(grad_out, unit_vals, inverse, gain_vec):
    scaled = grad_out * gain_vec
    centred = (
        scaled
        - jnp.mean(scaled, axis=-1, keepdims=True)
        - unit_vals * jnp.mean(scaled * unit_vals, axis=-1, keepdims=True)
    )
    return (inverse * centred, jnp.sum(grad_out * unit_vals, axis=0), jnp.sum(grad_out, axis=0))


def split_heads(packed):
    shaped = packed.reshape(packed.shape[0], packed.shape[1], 3, HEADS, HEAD_DIM)
    return (shaped[:, :, 0], shaped[:, :, 1], shaped[:, :, 2])


def attn_probs(queries, keys_part):
    scores = jnp.einsum(
        "iqhd,ikhd->ihqk", queries, keys_part, preferred_element_type=F32
    ) * HEAD_DIM ** (-0.5)
    exponent = jnp.exp(scores)
    return exponent / jnp.sum(exponent, axis=-1, keepdims=True)


def attention_forward(packed):
    queries, keys_part, values_part = split_heads(packed)
    probs_b = attn_probs(queries, keys_part).astype(BF)
    context = jnp.einsum("ihqk,ikhd->iqhd", probs_b, values_part, preferred_element_type=F32)
    return context.astype(BF).reshape(packed.shape[0], packed.shape[1], HEADS * HEAD_DIM)


def attention_backward(packed, d_context):
    queries, keys_part, values_part = split_heads(packed)
    probs = attn_probs(queries, keys_part)
    probs_b = probs.astype(BF)
    d_heads = d_context.reshape(packed.shape[0], packed.shape[1], HEADS, HEAD_DIM)
    d_values = jnp.einsum("ihqk,iqhd->ikhd", probs_b, d_heads, preferred_element_type=F32)
    d_probs = jnp.einsum("iqhd,ikhd->ihqk", d_heads, values_part, preferred_element_type=F32)
    row_dot = jnp.sum(probs * d_probs, axis=-1, keepdims=True)
    d_scores = (probs * (d_probs - row_dot)).astype(BF)
    scale = HEAD_DIM ** (-0.5)
    d_queries = jnp.einsum("ihqk,ikhd->iqhd", d_scores, keys_part, preferred_element_type=F32) * scale
    d_keys = jnp.einsum("ihqk,iqhd->ikhd", d_scores, queries, preferred_element_type=F32) * scale
    stacked = jnp.stack([d_queries, d_keys, d_values], axis=2)
    return stacked.astype(BF).reshape(packed.shape[0], packed.shape[1], 3 * HEADS * HEAD_DIM)


def nt(a, b):
    return lax.dot_general(a, b, (((1,), (1,)), ((), ())), preferred_element_type=F32)


def tn(a, b):
    return lax.dot_general(a, b, (((0,), (0,)), ((), ())), preferred_element_type=F32)


def nn(a, b):
    return jnp.dot(a, b, preferred_element_type=F32)


def picks_of(meta, first, cap, packet, lanes, at):
    spot = lax.broadcasted_iota(jnp.int32, (cap, packet), 0).astype(F32)
    found = []
    for k in range(2):
        route = meta[at : at + 1, k * lanes : k * lanes + packet]
        rank = meta[at + 1 : at + 2, k * lanes : k * lanes + packet]
        hits = [
            jnp.where((route == (first + j).astype(F32)) & (rank == spot), 1.0, 0.0) for j in range(EXP_DEV)
        ]
        found.append(jnp.concatenate(hits, axis=0))
    return found


def experts_back(tokens, cots, first_expert, w_in, w_out, router, rows, capacity, total_experts):
    count = len(tokens)
    n, packet, width = tokens[0].shape
    hidden = w_in.shape[2]
    images = count * n
    cap = round_up(capacity, 8)
    meta_at = rows // 8 * 8
    at = rows - meta_at
    lanes = round_up(rows, 128)
    m_rows = images * cap

    def kernel(first_ref, *refs):
        xs, cs = refs[:count], refs[count : 2 * count]
        win_ref, wout_ref, wr_ref = refs[2 * count : 2 * count + 3]
        yb_refs = refs[2 * count + 3 : 3 * count + 3]
        x_ref, act_ref, dpre_ref, de_ref, gate_ref, meta_ref = refs[3 * count + 3 : 3 * count + 9]
        xbuf, cbuf, xg, dg, yb, dgs, sems = refs[3 * count + 9 :]
        first = first_ref[0]

        def copies(p):
            return (
                pltpu.make_async_copy(cs[p], cbuf.at[p % 2], sems.at[0, p % 2]),
                pltpu.make_async_copy(xs[p], xbuf.at[p % 2], sems.at[1, p % 2]),
            )

        for p in range(2):
            for c in copies(p):
                c.start()
        for p in range(count):
            for c in copies(p):
                c.wait()
            for q in range(n):
                i = p * n + q
                meta = cbuf[p % 2, q, meta_at:packet, :]
                meta_ref[i] = meta
                p0, p1 = picks_of(meta.astype(F32), first, cap, packet, lanes, at)
                pick = (p0 + p1).astype(BF)
                xr = nn(pick, xbuf[p % 2, q])
                dr = nn(pick, cbuf[p % 2, q])
                for j in range(EXP_DEV):
                    xg[j, i * cap : (i + 1) * cap, :] = xr[j * cap : (j + 1) * cap]
                    dg[j, i * cap : (i + 1) * cap, :] = dr[j * cap : (j + 1) * cap]
            if p + 2 < count:
                for c in copies(p + 2):
                    c.start()
        def one_expert(j, carry):
            x = xg[j].astype(BF)
            d = dg[j]
            x_ref[j] = x
            logits = nn(x, wr_ref[...])
            lane = lax.broadcasted_iota(jnp.int32, logits.shape, 1)
            exponent = jnp.where(lane < total_experts, jnp.exp(logits), 0.0)
            chosen = jnp.sum(jnp.where(lane == first + j, exponent, 0.0), axis=1, keepdims=True)
            gate = chosen / jnp.sum(exponent, axis=1, keepdims=True)
            gate_ref[j] = jnp.broadcast_to(gate, (m_rows, 128))
            de_ref[j] = (gate * d).astype(BF)
            pre = nn(x, win_ref[j])
            squared = pre * pre
            t = jnp.tanh(GELU_C * pre * (1.0 + GELU_A * squared))
            half = 0.5 * (1.0 + t)
            act = (pre * half).astype(BF)
            act_ref[j] = act
            slope = half + 0.5 * pre * (1.0 - t * t) * (GELU_C * (1.0 + 3.0 * GELU_A * squared))
            dh = nt(d.astype(BF), wout_ref[j])
            dgs[j] = jnp.broadcast_to(jnp.sum(act.astype(F32) * dh, axis=1, keepdims=True), (m_rows, 128))
            d_pre = (slope * (gate * dh)).astype(BF)
            dpre_ref[j] = d_pre
            yb[j] = nt(d_pre, win_ref[j])
            return carry

        lax.fori_loop(0, EXP_DEV, one_expert, 0)
        for i in range(images):
            p0, p1 = picks_of(meta_ref[i].astype(F32), first, cap, packet, lanes, at)
            pick = (p0 + p1).astype(BF)
            mine = pl.ds(i * cap, cap)
            sb = jnp.concatenate([yb[j, mine, :] for j in range(EXP_DEV)], axis=0).astype(BF)
            sg = jnp.concatenate([dgs[j, mine, :] for j in range(EXP_DEV)], axis=0)[:, :1]
            back = tn(pick, sb)
            row0 = jnp.sum(p0 * sg, axis=0, keepdims=True)
            row1 = jnp.sum(p1 * sg, axis=0, keepdims=True)
            tail = back[meta_at:packet, :packet]
            r = lax.broadcasted_iota(jnp.int32, tail.shape, 0)
            tail = jnp.where(r == at, row0, jnp.where(r == at + 1, row1, tail))
            to = yb_refs[i // n]
            to[i % n] = back.astype(BF)
            to[i % n, meta_at:packet, :packet] = tail.astype(BF)

    hbm = pl.BlockSpec(memory_space=pl.ANY)
    vmem = pl.BlockSpec(memory_space=pltpu.VMEM)
    rows_bf = jax.ShapeDtypeStruct((EXP_DEV, m_rows, width), BF)
    hid_bf = jax.ShapeDtypeStruct((EXP_DEV, m_rows, hidden), BF)
    outs = pl.pallas_call(
        kernel,
        out_shape=tuple(jax.ShapeDtypeStruct(tokens[0].shape, BF) for _ in range(count))
        + (
            rows_bf,
            hid_bf,
            hid_bf,
            rows_bf,
            jax.ShapeDtypeStruct((EXP_DEV, m_rows, 128), F32),
            jax.ShapeDtypeStruct((images, packet - meta_at, width), BF),
        ),
        in_specs=[pl.BlockSpec(memory_space=pltpu.SMEM)] + [hbm] * (2 * count) + [vmem] * 3,
        out_specs=tuple([vmem] * (count + 6)),
        scratch_shapes=[
            pltpu.VMEM((2,) + tokens[0].shape, BF),
            pltpu.VMEM((2,) + tokens[0].shape, BF),
            pltpu.VMEM((EXP_DEV, m_rows, width), F32),
            pltpu.VMEM((EXP_DEV, m_rows, width), F32),
            pltpu.VMEM((EXP_DEV, m_rows, width), F32),
            pltpu.VMEM((EXP_DEV, m_rows, 128), F32),
            pltpu.SemaphoreType.DMA((2, 2)),
        ],
        cost_estimate=pl.CostEstimate(
            flops=8 * EXP_DEV * m_rows * width * hidden,
            transcendentals=EXP_DEV * m_rows * hidden,
            bytes_accessed=8 * images * packet * width,
        ),
        name="experts_back",
    )(first_expert, *tokens, *cots, w_in, w_out, router)
    return outs[:count], outs[count:]


def experts_out(saved, first_expert, w_out, count, packet, rows, capacity):
    _, act, _, _, gate, meta = saved
    m_rows, hidden = act.shape[1:]
    width = w_out.shape[2]
    images = meta.shape[0]
    n = images // count
    cap = round_up(capacity, 8)
    at = rows - rows // 8 * 8
    lanes = round_up(rows, 128)

    def kernel(first_ref, act_ref, gate_ref, meta_ref, wout_ref, *refs):
        outs, yo = refs[:count], refs[count]
        first = first_ref[0]
        for j in range(EXP_DEV):
            yo[j] = gate_ref[j][:, :1] * nn(act_ref[j], wout_ref[j])
        for i in range(images):
            p0, p1 = picks_of(meta_ref[i].astype(F32), first, cap, packet, lanes, at)
            mine = pl.ds(i * cap, cap)
            so = jnp.concatenate([yo[j, mine, :] for j in range(EXP_DEV)], axis=0).astype(BF)
            outs[i // n][i % n] = tn((p0 + p1).astype(BF), so).astype(BF)

    vmem = pl.BlockSpec(memory_space=pltpu.VMEM)
    return pl.pallas_call(
        kernel,
        out_shape=tuple(jax.ShapeDtypeStruct((n, packet, width), BF) for _ in range(count)),
        in_specs=[pl.BlockSpec(memory_space=pltpu.SMEM)] + [vmem] * 4,
        out_specs=tuple([vmem] * count),
        scratch_shapes=[pltpu.VMEM((EXP_DEV, m_rows, width), F32)],
        cost_estimate=pl.CostEstimate(
            flops=4 * EXP_DEV * m_rows * width * hidden,
            transcendentals=0,
            bytes_accessed=4 * images * packet * width,
        ),
        name="experts_out",
    )(first_expert, act, gate, meta, w_out)


def weight_grad(lefts, rights):
    count = len(lefts)
    _, m_rows, a = lefts[0].shape
    b = rights[0].shape[2]

    def kernel(*refs):
        total = tn(refs[0][0], refs[count][0])
        for i in range(1, count):
            total += tn(refs[i][0], refs[count + i][0])
        refs[2 * count][0] = total

    return pl.pallas_call(
        kernel,
        out_shape=jax.ShapeDtypeStruct((EXP_DEV, a, b), F32),
        grid=(EXP_DEV,),
        in_specs=[pl.BlockSpec((1, m_rows, a), lambda j: (j, 0, 0))] * count
        + [pl.BlockSpec((1, m_rows, b), lambda j: (j, 0, 0))] * count,
        out_specs=pl.BlockSpec((1, a, b), lambda j: (j, 0, 0)),
        cost_estimate=pl.CostEstimate(
            flops=2 * EXP_DEV * count * m_rows * a * b, transcendentals=0, bytes_accessed=EXP_DEV * a * b * 4
        ),
        name="weight_grad",
    )(*lefts, *rights)


def local(
    inputs, routes, ln1_gain, ln1_bias, w_qkv, w_attn_out, ln2_gain, ln2_bias, w_router, w_in, w_expert_out, cotangent
):
    row_count, width = inputs.shape
    experts_count, shard_count = lax.axis_size("expert"), lax.axis_size("shard")
    devices = experts_count * shard_count
    total_experts = EXP_DEV * experts_count
    capacity = max(2, 16 * row_count // (5 * total_experts))
    images = row_count // SEQ
    packet = round_up(row_count, 8)
    if packet - row_count < 2:
        packet += 8
    lanes = round_up(row_count, 128)
    dev_of_slot = slot_devices()

    small = jnp.concatenate([v[:, None] for v in (ln1_gain, ln1_bias, ln2_gain, ln2_bias)] + [w_router], axis=1)
    small_w = small.shape[1]
    small = jnp.pad(small, ((0, 0), (0, round_up(small_w, 128) - small_w)))
    w_packet = jnp.concatenate([w_qkv, w_attn_out, small], axis=1)
    w_pieces = [p for pieces in gather_core(gather_plane(w_packet, direct=True)) for p in pieces]
    widths = (3 * width, width, small.shape[1])
    full_qkv, full_attn_out, full_small = (
        t.reshape(width, -1) for t in place_blocks(w_pieces, dev_of_slot, devices, widths)
    )
    full_small = full_small[:, :small_w]
    full_ln1_gain, full_ln1_bias, full_ln2_gain, full_ln2_bias = (full_small[:, i] for i in range(4))
    full_router = full_small[:, 4:]

    experts = jnp.arange(total_experts, dtype=jnp.int32)[None, None, :]
    route_table = (routes[:, :, None] == experts).astype(F32)
    member = jnp.sum(route_table, axis=1)
    before = jnp.tril(jnp.ones((row_count, row_count), BF), -1)
    counts = jnp.dot(before, member.astype(BF), preferred_element_type=F32)
    ranks = jnp.sum(route_table * counts[:, None, :], axis=-1)
    pad_lane = ((0, 0), (0, lanes - row_count))
    meta = jnp.stack(
        [
            jnp.pad(routes.T.astype(F32), pad_lane, constant_values=-1.0).reshape(-1),
            jnp.pad(ranks.T, pad_lane, constant_values=-1.0).reshape(-1),
        ]
    )
    meta = jnp.pad(meta, ((0, packet - row_count - 2), (0, width - 2 * lanes))).astype(BF)
    cot_packet = jnp.concatenate([cotangent, meta], axis=0)
    cots = gather_plane(cot_packet)
    full_qkv, cots = lax.optimization_barrier((full_qkv, cots))
    cots = gather_core(cots)

    gain_one = full_ln1_gain.astype(F32)
    gain_two = full_ln2_gain.astype(F32)
    features = inputs.astype(F32)
    normed1, unit_one, inverse_one = layer_norm(features, gain_one, full_ln1_bias.astype(F32))
    narrow_one = normed1.astype(BF)
    packed = jnp.dot(narrow_one, full_qkv, preferred_element_type=F32).astype(BF)
    packed_images = packed.reshape(images, SEQ, 3 * width)
    context = attention_forward(packed_images).reshape(row_count, width)
    hidden = features + jnp.dot(context, full_attn_out, preferred_element_type=F32)
    normed2, unit_two, inverse_two = layer_norm(hidden, gain_two, full_ln2_bias.astype(F32))
    narrow_two = normed2.astype(BF)

    tokens = gather_core(
        gather_plane(jnp.pad(narrow_two, ((0, packet - row_count), (0, 0)))), in_turn=True
    )
    router_wide = jnp.pad(full_router, ((0, 0), (0, 128 - total_experts)))
    first_expert = (lax.axis_index("expert") * EXP_DEV).astype(jnp.int32).reshape(1)
    backs, saves = [], []
    for x, c in zip(tokens, cots):
        back, saved = experts_back(
            x, c, first_expert, w_in, w_expert_out, router_wide, row_count, capacity, total_experts
        )
        backs.append(back)
        saves.append(saved)
    back_parts = scatter_plane(backs)
    back_sum = scatter_shard(back_parts)
    late, _ = lax.optimization_barrier((saves, back_parts))
    pieces = len(tokens[0])
    out_sum = scatter_shard(
        scatter_plane(
            [experts_out(saved, first_expert, w_expert_out, pieces, packet, row_count, capacity) for saved in late]
        )
    )
    grad_w_in = weight_grad([v[0] for v in saves], [v[2] for v in saves])
    grad_w_expert_out = weight_grad([v[1] for v in saves], [v[3] for v in saves])

    logits = jnp.dot(narrow_two, full_router, preferred_element_type=F32)
    exponent = jnp.exp(logits)
    router_probs = exponent / jnp.sum(exponent, axis=-1, keepdims=True)
    outputs = (hidden + out_sum[:row_count]).astype(BF)
    d_gate = back_sum[row_count : row_count + 2, :row_count].T
    grad_out = cotangent.astype(F32)
    d_probs = jnp.sum(route_table * d_gate[:, :, None], axis=1)
    d_logits = router_probs * (d_probs - jnp.sum(router_probs * d_probs, axis=-1, keepdims=True))
    grad_router = jnp.dot(narrow_two.astype(F32).T, d_logits, precision=lax.Precision.HIGHEST)
    d_normed2 = back_sum[:row_count] + jnp.dot(
        d_logits, full_router.astype(F32).T, precision=lax.Precision.HIGHEST
    )
    d_norm_two, grad_gain_two, grad_bias_two = norm_back(d_normed2, unit_two, inverse_two, gain_two)
    d_hidden = grad_out + d_norm_two
    d_hidden_b = d_hidden.astype(BF)
    grad_attn_out = jnp.dot(context.T, d_hidden_b, preferred_element_type=F32)
    d_context = jnp.dot(d_hidden_b, full_attn_out.T, preferred_element_type=F32).astype(BF)
    d_packed = attention_backward(packed_images, d_context.reshape(images, SEQ, width)).reshape(
        row_count, 3 * width
    )
    grad_qkv = jnp.dot(narrow_one.T, d_packed, preferred_element_type=F32)
    d_normed1 = jnp.dot(d_packed, full_qkv.T, preferred_element_type=F32)
    d_norm_one, grad_gain_one, grad_bias_one = norm_back(d_normed1, unit_one, inverse_one, gain_one)
    grad_inputs = d_hidden + d_norm_one

    grad_small = jnp.concatenate(
        [v[:, None] for v in (grad_gain_one, grad_bias_one, grad_gain_two, grad_bias_two)] + [grad_router], axis=1
    )
    grad_small = jnp.pad(grad_small, ((0, 0), (0, round_up(small_w, 128) - small_w)))
    tables = [g.astype(BF).reshape(devices, width // devices, -1) for g in (grad_qkv, grad_attn_out, grad_small)]
    sizes = [[len(p) for p in pieces] for pieces in chunk_labels()]
    blocks = list(take_blocks(tables, dev_of_slot, sum(sizes, [])))
    grads = []
    for group in sizes:
        grads.append(blocks[: len(group)])
        blocks = blocks[len(group) :]
    own = scatter_shard(scatter_plane(grads), direct=True)
    own_small = own[:, 4 * width :]
    return (
        outputs,
        grad_inputs,
        own_small[:, 0],
        own_small[:, 1],
        own[:, : 3 * width],
        own[:, 3 * width : 4 * width],
        own_small[:, 2],
        own_small[:, 3],
        own_small[:, 4:small_w],
        grad_w_in,
        grad_w_expert_out,
    )


def solution(mesh):
    rows, vec = P(AXES, None), P(AXES)
    placed = (rows, rows, vec, vec, rows, rows, vec, vec, rows, P("expert", None, "shard"), P("expert", "shard", None), rows)
    outs = (rows, rows, vec, vec, rows, rows, vec, vec, rows, P("expert", None, "shard"), P("expert", "shard", None))
    return jax.shard_map(local, mesh=mesh, in_specs=placed, out_specs=outs, check_vma=False)
```
